32 devices in a mesh: row: 4 (over y, x), col: 8 (over z, core).
Axes of the slice: x: 2, y: 2, z: 4, core: 2. Of those that a mesh axis runs over, the one named last changes fastest.
Arguments:
- covariance: float32 [64, 128, 64, 128], P('row', None, 'col'), may hold values from -1 to 4, as said below
- wind_x: float32 [64, 128], replicated, may hold values from -0.2 to 0.2
- wind_y: float32 [64, 128], replicated, may hold values from -0.2 to 0.2
- diffusivity: float32 [64, 128], replicated, may hold values from 0.1 to 0.2
- obs_point: int32 [512], replicated, may hold values from 0 to 8191, as said below
- obs_var: float32 [512], replicated, may hold values from 0.3 to 1
Outputs:
- analysis: float32 [64, 128, 64, 128], P('row', None, 'col')
The draws below stay inside these ranges and needn't reach their ends.
Inputs may be any that keep to these rules, and one draw needn't show every extreme that they name: `covariance`: symmetric and positive definite. `obs_point`: distinct and ascending; at most 128 of them lie in one aligned block of 1024 points and some block holds exactly 128; at most 256 lie in one aligned block of 2048 points and some block holds exactly 256.
All inputs are finite; a program needn't handle non-finite values.
Results may differ from the reference program's by a relative error of at most 0.0001.
Values sent between devices are 32-bit elements; how exact they have to be, the bound alone decides.
A program may use at most 128 MiB of HBM per device.

```python
import math
import jax
import jax.numpy as jnp
from jax import lax

GY = 64
GX = 128
NOBS = 512
STEPS = 2
NS_ITERS = 4
NPTS = 8192
ROWS_DEV = 2048
COLS_DEV = 1024
MAXC = 128


def draw_covariance(key, part):
    noise_key, diag_key = jax.random.split(jax.random.fold_in(key, 11))
    noise = jax.random.normal(noise_key, (GY, GX, GY, GX), jnp.float32)
    symmetric = (noise + noise.transpose(2, 3, 0, 1)) * (0.25 / math.sqrt(GY * GX))
    diagonal = jax.random.uniform(diag_key, (GY, GX), jnp.float32, 1.0, 3.0)
    same_y = jnp.arange(GY)[:, None, None, None] == jnp.arange(GY)[None, None, :, None]
    same_x = jnp.arange(GX)[None, :, None, None] == jnp.arange(GX)[None, None, None, :]
    identity = (same_y & same_x).astype(jnp.float32)
    return symmetric + identity * diagonal[:, :, None, None]


def draw_obs_point(key, part):
    full_key, slot_key, point_key = jax.random.split(jax.random.fold_in(key, 7), 3)
    col_blocks = NPTS // COLS_DEV
    row_blocks = NPTS // ROWS_DEV
    per_row = col_blocks // row_blocks
    full_row = jax.random.randint(full_key, (), 0, row_blocks)
    slot_block = jnp.arange(col_blocks * MAXC, dtype=jnp.int32) // MAXC
    slot_full = slot_block // per_row == full_row
    score = jax.random.permutation(slot_key, col_blocks * MAXC).astype(jnp.int32)
    score = jnp.where(slot_full, -1, score)
    order = jnp.argsort(score, stable=True)
    taken = jnp.zeros((col_blocks * MAXC,), jnp.int32).at[order[:NOBS]].set(1)
    block_counts = jnp.sum(taken.reshape(col_blocks, MAXC), axis=1)
    limit = 2 ** 30 // COLS_DEV
    point_score = jax.random.randint(point_key, (col_blocks, COLS_DEV), 0, limit) * COLS_DEV + jnp.arange(COLS_DEV, dtype=jnp.int32)[None, :]
    ranks = jnp.argsort(jnp.argsort(point_score, axis=1), axis=1)
    chosen = (ranks < block_counts[:, None]).reshape(-1)
    return jnp.nonzero(chosen, size=NOBS)[0].astype(jnp.int32)


def setup_inputs(seed: int = 0) -> dict:
    keys = jax.random.split(jax.random.key(seed), 7)
    covariance = draw_covariance(jax.random.fold_in(keys[6], 71), 0)
    wind_x = jnp.clip(jax.random.uniform(keys[1], (GY, GX), jnp.float32, -0.2, 0.2), -0.2, 0.2)
    wind_y = jnp.clip(jax.random.uniform(keys[2], (GY, GX), jnp.float32, -0.2, 0.2), -0.2, 0.2)
    diffusivity = jnp.clip(jax.random.uniform(keys[3], (GY, GX), jnp.float32, 0.1, 0.2), 0.1, 0.2)
    obs_point = draw_obs_point(jax.random.fold_in(keys[6], 71), 0)
    obs_var = jnp.clip(jnp.exp(jax.random.uniform(keys[5], (NOBS,), jnp.float32, math.log(0.3), math.log(1.0))), 0.3, 1.0)
    return dict(covariance=covariance, wind_x=wind_x, wind_y=wind_y, diffusivity=diffusivity, obs_point=obs_point, obs_var=obs_var)


newton_scale = 4.0


def stencil_weights(wind_x, wind_y, diffusivity):
    return (1.0 - 4.0 * diffusivity, diffusivity - 0.5 * wind_x, diffusivity + 0.5 * wind_x,
            diffusivity - 0.5 * wind_y, diffusivity + 0.5 * wind_y)


def apply_first(extended, weights):
    inner = extended[1:-1]
    w_centre, w_east, w_west, w_north, w_south = [w_table[1:-1, :, None, None] for w_table in weights]
    return (w_centre * inner + w_east * jnp.roll(inner, -1, axis=1) + w_west * jnp.roll(inner, 1, axis=1)
            + w_north * extended[2:] + w_south * extended[:-2])


def apply_second(extended, weights):
    inner = extended[:, :, 1:-1]
    w_centre, w_east, w_west, w_north, w_south = [w_table[None, None, 1:-1, :] for w_table in weights]
    return (w_centre * inner + w_east * jnp.roll(inner, -1, axis=3) + w_west * jnp.roll(inner, 1, axis=3)
            + w_north * extended[:, :, 2:] + w_south * extended[:, :, :-2])


def reference(covariance, wind_x, wind_y, diffusivity, obs_point, obs_var):
    padded = tuple(jnp.pad(w_table, ((1, 1), (0, 0))) for w_table in stencil_weights(wind_x, wind_y, diffusivity))
    transported = covariance
    for step_index in range(STEPS):
        transported = apply_first(jnp.pad(transported, ((1, 1), (0, 0), (0, 0), (0, 0))), padded)
        transported = apply_second(jnp.pad(transported, ((0, 0), (0, 0), (1, 1), (0, 0))), padded)
    flat_matrix = transported.reshape(NPTS, NPTS)
    obs_rows = jnp.take(flat_matrix, obs_point, axis=0)
    obs_cols = jnp.take(flat_matrix, obs_point, axis=1)
    innovation = jnp.take(obs_rows, obs_point, axis=1) + jnp.diag(obs_var)
    inverse = jnp.eye(NOBS, dtype=jnp.float32) / newton_scale
    for sweep_index in range(NS_ITERS):
        product = jnp.dot(innovation, inverse, precision=lax.Precision.HIGHEST)
        inverse = 2.0 * inverse - jnp.dot(inverse, product, precision=lax.Precision.HIGHEST)
    gain = jnp.dot(obs_cols, inverse, precision=lax.Precision.HIGHEST)
    analysis = flat_matrix - jnp.dot(gain, obs_rows, precision=lax.Precision.HIGHEST)
    return analysis.reshape(GY, GX, GY, GX)
```

```python
import functools

import jax
import jax.numpy as jnp
from jax import lax
from jax.experimental import pallas as pl
from jax.experimental.pallas import tpu as pltpu
from jax.sharding import PartitionSpec as P

STEPS = 2
NS_ITERS = 4
newton_scale = 4.0
OFFSETS = ((0, 0), (0, 1), (0, -1), (1, 0), (-1, 0))


def stencil_weights(wind_x, wind_y, diffusivity):
    return (
        1.0 - 4.0 * diffusivity,
        diffusivity - 0.5 * wind_x,
        diffusivity + 0.5 * wind_x,
        diffusivity - 0.5 * wind_y,
        diffusivity + 0.5 * wind_y,
    )


def shifted(table, dy, dx):
    table = jnp.roll(table, -dx, axis=1) if dx else table
    if dy == 1:
        return jnp.pad(table[1:], ((0, 1), (0, 0)))
    if dy == -1:
        return jnp.pad(table[:-1], ((1, 0), (0, 0)))
    return table


def squared_weights(weights):
    out = {}
    for first, (dy1, dx1) in enumerate(OFFSETS):
        for second, (dy2, dx2) in enumerate(OFFSETS):
            term = weights[first] * shifted(weights[second], dy1, dx1)
            key = (dy1 + dy2, dx1 + dx2)
            out[key] = out[key] + term if key in out else term
    return out


def split(value):
    high = value.astype(jnp.bfloat16)
    return high, (value - high.astype(jnp.float32)).astype(jnp.bfloat16)


def band_blocks(squared, first_row, length, grid_x, transposed):
    pair = STEPS * grid_x
    pairs = length // STEPS
    shape = (pairs, 3, pair, pair)
    target_dim, source_dim = (3, 2) if transposed else (2, 3)
    target = lax.broadcasted_iota(jnp.int32, shape, target_dim)
    source = lax.broadcasted_iota(jnp.int32, shape, source_dim)
    which = lax.broadcasted_iota(jnp.int32, shape, 1)
    dy = STEPS * (which - 1) + source // grid_x - target // grid_x
    dx = (source % grid_x - target % grid_x + grid_x // 2) % grid_x - grid_x // 2
    code = dy * grid_x + dx
    total = jnp.zeros(shape, jnp.float32)
    for (key_y, key_x), table in squared.items():
        rows = lax.dynamic_slice_in_dim(table, first_row, length, 0).reshape(pairs, pair)
        rows = rows[:, None, None, :] if transposed else rows[:, None, :, None]
        total = jnp.where(code == key_y * grid_x + key_x, rows, total)
    high = lax.reduce_precision(total, 8, 7)
    return high.astype(jnp.bfloat16), (total - high).astype(jnp.bfloat16)


def dot3(a, b, dims=(((1,), (0,)), ((), ()))):
    out = None
    for left, right in ((a[0], b[0]), (a[0], b[1]), (a[1], b[0])):
        term = lax.dot_general(left, right, dims, preferred_element_type=jnp.float32)
        out = term if out is None else out + term
    return out


def transport_kernel(
    blocks,
    col_blocks,
    pair,
    centre_ref,
    west_ref,
    east_ref,
    ends_ref,
    a_hi,
    a_lo,
    b_hi,
    b_lo,
    row_loc,
    col_loc,
    out_ref,
    rows_ref,
    cols_ref,
    ring_hi,
    ring_lo,
):
    step = pl.program_id(0)
    slot = lax.rem(step, 3)
    cols = col_blocks * pair
    inside = (step >= 1) & (step <= blocks)

    def put(first, value):
        high, low = split(value)
        ring_hi[slot, :, first : first + value.shape[1]] = high
        ring_lo[slot, :, first : first + value.shape[1]] = low

    @pl.when(inside)
    def _():
        put(pair, centre_ref[...])

    @pl.when(jnp.logical_not(inside))
    def _():
        put(pair, ends_ref[0])

    put(0, west_ref[...])
    put(pair + cols, east_ref[...])

    @pl.when(step == 0)
    def _():
        rows_ref[...] = jnp.zeros_like(rows_ref)

    @pl.when(step >= 2)
    def _():
        mid = None
        for which in range(3):
            source = lax.rem(step + 1 + which, 3)
            term = dot3((a_hi[0, which], a_lo[0, which]), (ring_hi[source], ring_lo[source]))
            mid = term if mid is None else mid + term
        mid_hi, mid_lo = split(mid)
        for block in range(col_blocks):
            first = block * pair
            total = None
            for which in range(3):
                at = first + which * pair
                term = dot3(
                    (mid_hi[:, at : at + pair], mid_lo[:, at : at + pair]),
                    (b_hi[block, which], b_lo[block, which]),
                )
                total = term if total is None else total + term
            out_ref[:, first : first + pair] = total
        high, low = split(out_ref[...])
        row_at = lax.broadcasted_iota(jnp.int32, (row_loc.shape[0], pair), 1)
        row_hot = (row_at + (step - 2) * pair == row_loc[...]).astype(jnp.float32)
        row_hot = row_hot.astype(jnp.bfloat16)
        rows_ref[...] += jnp.dot(row_hot, high, preferred_element_type=jnp.float32) + jnp.dot(
            row_hot, low, preferred_element_type=jnp.float32
        )
        col_at = lax.broadcasted_iota(jnp.int32, (col_loc.shape[0], cols), 1)
        col_hot = (col_at == col_loc[...]).astype(jnp.float32).astype(jnp.bfloat16)
        dims = (((1,), (1,)), ((), ()))
        cols_ref[...] = lax.dot_general(
            col_hot, high, dims, preferred_element_type=jnp.float32
        ) + lax.dot_general(col_hot, low, dims, preferred_element_type=jnp.float32)


def transport(tile, west, east, ends, a, b, row_loc, col_loc, pair):
    rows, cols = tile.shape
    blocks, col_blocks = rows // pair, cols // pair
    max_row, max_col = row_loc.shape[0], col_loc.shape[0]
    centre_at = lambda k: (jnp.clip(k - 1, 0, blocks - 1), 0)
    band_at = lambda k: (jnp.maximum(k - 2, 0), 0, 0, 0)
    whole4 = lambda k: (0, 0, 0, 0)
    whole2 = lambda k: (0, 0)
    return pl.pallas_call(
        functools.partial(transport_kernel, blocks, col_blocks, pair),
        grid=(blocks + 2,),
        in_specs=[
            pl.BlockSpec((pair, cols), centre_at),
            pl.BlockSpec((pair, pair), lambda k: (k, 0)),
            pl.BlockSpec((pair, pair), lambda k: (k, 0)),
            pl.BlockSpec((1, pair, cols), lambda k: (jnp.where(k == 0, 0, 1), 0, 0)),
            pl.BlockSpec((1, 3, pair, pair), band_at),
            pl.BlockSpec((1, 3, pair, pair), band_at),
            pl.BlockSpec((col_blocks, 3, pair, pair), whole4),
            pl.BlockSpec((col_blocks, 3, pair, pair), whole4),
            pl.BlockSpec((max_row, 1), whole2),
            pl.BlockSpec((max_col, 1), whole2),
        ],
        out_specs=[
            pl.BlockSpec((pair, cols), lambda k: (jnp.maximum(k - 2, 0), 0)),
            pl.BlockSpec((max_row, cols), whole2),
            pl.BlockSpec((max_col, pair), lambda k: (0, jnp.maximum(k - 2, 0))),
        ],
        out_shape=[
            jax.ShapeDtypeStruct((rows, cols), jnp.float32),
            jax.ShapeDtypeStruct((max_row, cols), jnp.float32),
            jax.ShapeDtypeStruct((max_col, rows), jnp.float32),
        ],
        scratch_shapes=[
            pltpu.VMEM((3, pair, cols + 2 * pair), jnp.bfloat16),
            pltpu.VMEM((3, pair, cols + 2 * pair), jnp.bfloat16),
        ],
        compiler_params=pltpu.CompilerParams(vmem_limit_bytes=48 << 20),
    )(tile, west, east, ends, *a, *b, row_loc, col_loc)


def on_device(covariance, wind_x, wind_y, diffusivity, obs_point, obs_var):
    rows_grid, grid_x, cols_grid, _ = covariance.shape
    row_count, col_count = lax.axis_size("row"), lax.axis_size("col")
    row_index, col_index = lax.axis_index("row"), lax.axis_index("col")
    rows_dev, cols_dev = rows_grid * grid_x, cols_grid * grid_x
    pair = STEPS * grid_x
    obs_total = obs_point.shape[0]
    tile = covariance.reshape(rows_dev, cols_dev)

    def fetch(value, dy, dx):
        moves = []
        for row in range(row_count):
            for col in range(col_count):
                if 0 <= row + dy < row_count and 0 <= col + dx < col_count:
                    moves.append(
                        ((row + dy) * col_count + col + dx, row * col_count + col)
                    )
        return lax.ppermute(value, ("row", "col"), moves)

    top, bottom = tile[:pair], tile[rows_dev - pair :]
    west = fetch(tile[:, cols_dev - pair :], 0, -1)
    east = fetch(tile[:, :pair], 0, 1)
    north = fetch(bottom, -1, 0)
    south = fetch(top, 1, 0)
    north_west = fetch(bottom[:, cols_dev - pair :], -1, -1)
    north_east = fetch(bottom[:, :pair], -1, 1)
    south_west = fetch(top[:, cols_dev - pair :], 1, -1)
    south_east = fetch(top[:, :pair], 1, 1)
    squared = squared_weights(stencil_weights(wind_x, wind_y, diffusivity))
    a = band_blocks(squared, row_index * rows_grid, rows_grid, grid_x, False)
    b = band_blocks(squared, col_index * cols_grid, cols_grid, grid_x, True)

    max_row = 2 * obs_total // row_count
    max_col = 2 * obs_total // col_count
    obs_ids = jnp.arange(obs_total, dtype=jnp.int32)
    row_base, col_base = row_index * rows_dev, col_index * cols_dev

    def local(base, size, limit):
        start = jnp.sum((obs_point < base).astype(jnp.int32))
        padded = jnp.pad(obs_point, (0, limit), constant_values=-1)
        point = lax.dynamic_slice_in_dim(padded, start, limit, 0) - base
        return jnp.where((point >= 0) & (point < size), point, -1)

    def slot_of(size, limit):
        owner = obs_point // size
        start = jnp.sum(
            (obs_point[None, :] < (owner * size)[:, None]).astype(jnp.int32), axis=1
        )
        return owner, obs_ids - start

    row_loc = local(row_base, rows_dev, max_row)
    col_loc = local(col_base, cols_dev, max_col)
    row_owner, row_at = slot_of(rows_dev, max_row)
    col_owner, col_at = slot_of(cols_dev, max_col)
    row_slot = ((row_owner - row_index) % row_count) * max_row + row_at
    near_slot = ((col_owner - col_index) % col_count) * max_col + col_at
    col_slot = col_owner * max_col + col_at

    def exchanged(part, axis, count):
        parts = [part]
        for hop in range(1, count):
            moves = [((me + hop) % count, me) for me in range(count)]
            parts.append(lax.ppermute(part, axis, moves))
        return jnp.concatenate(parts, axis=0)

    flat_tile, rows_part, cols_part = transport(
        tile,
        jnp.concatenate([north_west, west, south_west], axis=0),
        jnp.concatenate([north_east, east, south_east], axis=0),
        jnp.stack([north, south]),
        a,
        b,
        row_loc[:, None],
        col_loc[:, None],
        pair,
    )
    rows_all = exchanged(rows_part, "row", row_count)
    cols_all = lax.all_gather(cols_part, "col", axis=0, tiled=True)
    high = lax.Precision.HIGH
    obs_rows = jnp.take(rows_all, row_slot, axis=0, mode="clip")
    col_hot = (col_loc[:, None] == jnp.arange(cols_dev, dtype=jnp.int32)[None, :]).astype(
        jnp.float32
    )
    dims = (((1,), (1,)), ((), ()))
    pairs_part = lax.dot_general(col_hot, obs_rows, dims, precision=lax.Precision.HIGHEST)
    pairs_all = exchanged(pairs_part, "col", col_count)
    innovation = jnp.take(pairs_all, near_slot, axis=0, mode="clip").T + jnp.diag(obs_var)
    inverse = jnp.eye(obs_total, dtype=jnp.float32) / newton_scale
    for sweep_index in range(NS_ITERS):
        product = jnp.dot(innovation, inverse, precision=lax.Precision.HIGHEST)
        inverse = 2.0 * inverse - jnp.dot(inverse, product, precision=lax.Precision.HIGHEST)
    scaled = jnp.dot(inverse, obs_rows, precision=high)
    slot_ids = jnp.arange(max_col * col_count, dtype=jnp.int32)
    spread = (slot_ids[:, None] == col_slot[None, :]).astype(jnp.float32)
    scaled = jnp.dot(spread, scaled, precision=high)
    dims = (((0,), (0,)), ((), ()))
    analysis = flat_tile - lax.dot_general(cols_all, scaled, dims, precision=high)
    return analysis.reshape(rows_grid, grid_x, cols_grid, grid_x)


def solution(mesh):
    in_specs = (P("row", None, "col", None), P(), P(), P(), P(), P())
    out_specs = P("row", None, "col", None)
    return jax.shard_map(
        on_device, mesh=mesh, in_specs=in_specs, out_specs=out_specs, check_vma=False
    )
```
